256 devices in a mesh: tiles: 64 (over z, x, core), rep: 4 (over y).
Axes of the slice: x: 4, y: 4, z: 8, core: 2. Of those that a mesh axis runs over, the one named last changes fastest.
Arguments:
- affinity: bfloat16 [1024, 512, 512], P(('tiles', 'rep')), may hold values from -0.25 to 0.25
- tile_pairs: int32 [1024, 2], P(('tiles', 'rep')), may hold values from 0 to 255, as said below
- factors: float32 [256, 512, 256], P('tiles'), may hold values from -6 to 6
Outputs:
- polar_factors: float32 [256, 512, 256], P('tiles')
The draws below stay inside these ranges and needn't reach their ends.
Inputs may be any that keep to these rules, and one draw needn't show every extreme that they name: `tile_pairs`: column 0 of a row is an image owned by the index of tiles that holds the row (images o * 4 to (o + 1) * 4 - 1 belong to index o); column 1 differs from column 0 by 1 to 4, and by exactly 4 in the first row held by every index of tiles.
All inputs are finite; a program needn't handle non-finite values.
Results may differ from the reference program's by a relative error of at most 0.0022.
Values may be sent and summed in bfloat16 or wider, within the bound.
No kernel may reach another device: no remote copies, remote signals or barrier semaphores. Data moves between devices by JAX's collectives and lax.ppermute only.
A program may use at most 64 MiB of HBM per device.

```python
import math
import jax
import jax.numpy as jnp
from jax import lax

P_SIZE = 512
U = 256
IMG_DEV = 4
ROUNDS = 1
NS_STEPS = 6
IMAGES = 256
TILES = 1024


def draw_tile_pairs(key, part):
    per_owner = TILES // (IMAGES // IMG_DEV)
    row_ids = jnp.arange(TILES, dtype=jnp.int32)
    owner = row_ids // per_owner
    keys = jax.random.split(jax.random.fold_in(key, 11), 4)
    first_pick = jnp.minimum(jax.random.randint(keys[0], (TILES,), 0, IMG_DEV), jax.random.randint(keys[1], (TILES,), 0, IMG_DEV))
    first_image = owner * IMG_DEV + first_pick
    offset = jax.random.randint(keys[2], (TILES,), 1, IMG_DEV + 1)
    offset = jnp.where(row_ids % per_owner == 0, IMG_DEV, offset)
    direction = jax.random.randint(keys[3], (TILES,), 0, 2) * 2 - 1
    second_image = first_image + direction * offset
    outside = (second_image < 0) | (second_image >= IMAGES)
    second_image = jnp.where(outside, first_image - direction * offset, second_image)
    return jnp.stack([first_image, second_image], axis=1).astype(jnp.int32)


def draw_factors(key, part):
    keys = jax.random.split(jax.random.fold_in(key, 23), 1)
    values = jax.random.normal(keys[0], (IMAGES, P_SIZE, U), jnp.float32)
    return jnp.clip(values, -6.0, 6.0)


def levels(rng, dims, cuts, low, largest):
    gain = 1.0
    for position, blocks in cuts:
        steps = jax.random.uniform(jax.random.fold_in(jax.random.fold_in(rng, 6), position), (blocks,), jnp.float32, low / len(cuts), largest / len(cuts))
        gain = gain * jnp.repeat(jnp.exp(steps), dims[position] // blocks).reshape((-1,) + (1,) * (len(dims) - 1 - position))
    return gain


def normal_values(own_key, shape, deviation, limit, cuts=(), held_as=jnp.bfloat16):
    result = deviation * jax.random.normal(own_key, shape, jnp.float32)
    if cuts:
        result = result * levels(own_key, shape, cuts, -0.22, 0.18)
    return jnp.clip(result, -limit, limit).astype(held_as)


def setup_inputs(seed: int = 0) -> dict:
    seeds = jax.random.split(jax.random.key(seed), 4)
    affinity = normal_values(seeds[0], (TILES, P_SIZE, P_SIZE), P_SIZE ** -0.5, 0.25, ((0, 256),))
    tile_pairs = draw_tile_pairs(jax.random.fold_in(seeds[3], 71), 0)
    factors = draw_factors(jax.random.fold_in(seeds[3], 71), 0)
    return dict(affinity=affinity, tile_pairs=tile_pairs, factors=factors)


epsilon = 1e-06
start_scale = 0.25
ascent_step = 0.25

def polar_project(ascended):
    iterate = ascended
    for sweep_index in range(NS_STEPS):
        gram_matrix = jnp.einsum('npu,npv->nuv', iterate, iterate, precision=lax.Precision.HIGHEST)
        if sweep_index == 0:
            squares = jnp.trace(gram_matrix, axis1=1, axis2=2)[:, None, None]
            factor = start_scale * math.sqrt(iterate.shape[2]) * lax.rsqrt(squares + epsilon)
            iterate = iterate * factor
            gram_matrix = gram_matrix * (factor * factor)
        iterate = 1.5 * iterate - 0.5 * jnp.einsum('npu,nuv->npv', iterate, gram_matrix, precision=lax.Precision.HIGHEST)
    return iterate * math.sqrt(P_SIZE)

def reference(affinity, tile_pairs, factors):
    current = factors
    for round_index in range(ROUNDS):
        rounded = current.astype(jnp.bfloat16)

        def accumulate(total, item):
            tile, pair = item
            first_image = lax.dynamic_index_in_dim(rounded, pair[0], 0, keepdims=False)
            second_image = lax.dynamic_index_in_dim(rounded, pair[1], 0, keepdims=False)
            forward = jnp.dot(tile, second_image, preferred_element_type=jnp.float32)
            backward = jnp.dot(tile.T, first_image, preferred_element_type=jnp.float32)
            total = total.at[pair[0]].add(forward)
            total = total.at[pair[1]].add(backward)
            return (total, None)
        gradient, unused = lax.scan(accumulate, jnp.zeros(current.shape, jnp.float32), (affinity, tile_pairs))
        current = polar_project(current + ascent_step * gradient)
    return current
```

```python
import functools
import math

import jax
import jax.numpy as jnp
from jax import lax
from jax.experimental import pallas as pl
from jax.experimental.pallas import tpu as pltpu
from jax.sharding import PartitionSpec as P

P_SIZE = 512
NS_STEPS = 6
WIDE_STEPS = 2

epsilon = 1e-06
start_scale = 0.25
ascent_step = 0.25


SMEM = pl.BlockSpec(memory_space=pltpu.SMEM)
VMEM = pl.BlockSpec(memory_space=pltpu.VMEM)
MIB = 1 << 20


def mate(x):
    n = lax.axis_size("tiles")
    return lax.ppermute(x, "tiles", [(i, i ^ 1) for i in range(n)])


def across(x):
    n = lax.axis_size("tiles")
    pairs = [(i, i + 1) for i in range(1, n - 1, 2)]
    return lax.ppermute(x, "tiles", pairs + [(b, a) for a, b in pairs])


def turned(x, by):
    n = lax.axis_size("rep")
    return lax.ppermute(x, "rep", [(i, (i + by) % n) for i in range(n)])


def dot(a, b, dims=((1,), (0,))):
    return lax.dot_general(a, b, (dims, ((), ())), preferred_element_type=jnp.float32)


TN = ((0,), (0,))


def accumulate(acc, slot, fresh, term):
    acc[slot] = jnp.where(fresh, jnp.zeros_like(term), acc[slot]) + term


def backward_kernel(meta, affinity, rounded, own, to_mate, c0, c1, c2, c3, acc):
    tiles = affinity.shape[0]
    images = rounded.shape[0]
    slots = [meta[tiles + t] for t in range(tiles)]
    for t in range(tiles):
        fresh = slots[t] >= 0
        for u in range(t):
            fresh = jnp.logical_and(fresh, slots[u] != slots[t])
        accumulate(acc, slots[t], fresh, dot(affinity[t], rounded[meta[t]], TN))

    def total(slot):
        hit = slots[0] == slot
        for t in range(1, tiles):
            hit = jnp.logical_or(hit, slots[t] == slot)
        value = acc[slot]
        return jnp.where(hit, value, jnp.zeros_like(value))

    for k, ref in enumerate((c0, c1, c2, c3)):
        ref[...] = total(meta[2 * tiles + k]).astype(ref.dtype)
    for j in range(images):
        to_mate[j] = total(2 * images + j).astype(to_mate.dtype)
    for j in range(images):
        own[j] = total(images + j)


def forward_kernel(meta, affinity, rounded, from_mate, from_across, own, terms, p0, p1, p2, p3, rhs, acc):
    tiles = affinity.shape[0]
    images = rounded.shape[0]
    for j in range(images):
        acc[j] = own[j] + terms[j].astype(jnp.float32)
    for t in range(tiles):
        slot = meta[tiles + t]

        @pl.when(slot < images)
        def _():
            rhs[...] = from_across[slot]

        @pl.when(jnp.logical_and(slot >= images, slot < 2 * images))
        def _():
            rhs[...] = rounded[slot - images]

        @pl.when(slot >= 2 * images)
        def _():
            rhs[...] = from_mate[slot - 2 * images]

        first = meta[t]
        acc[first] = acc[first] + dot(affinity[t], rhs[...])
    for k, ref in enumerate((p0, p1, p2, p3)):
        ref[...] = acc[meta[2 * tiles + k]].astype(ref.dtype)


def split(x):
    high = x.astype(jnp.bfloat16)
    return high, (x - high.astype(jnp.float32)).astype(jnp.bfloat16)


def project_kernel(index, factors, gradient, *rest):
    out = rest[-1]
    x = factors[0] + ascent_step * gradient[...].astype(jnp.float32)
    squares = jnp.sum(jnp.sum(x * x, axis=0, keepdims=True), axis=1, keepdims=True)
    x = x * (start_scale * math.sqrt(x.shape[1]) * lax.rsqrt(squares + epsilon))
    for step in range(NS_STEPS):
        if step < NS_STEPS - WIDE_STEPS:
            high = x.astype(jnp.bfloat16)
            gram = dot(high, high, TN)
            change = dot(high, gram.astype(jnp.bfloat16))
        else:
            high, low = split(x)
            gram = dot(high, high, TN) + (dot(high, low, TN) + dot(low, high, TN))
            g_high, g_low = split(gram)
            change = dot(high, g_high) + (dot(high, g_low) + dot(low, g_high))
        x = 1.5 * x - 0.5 * change
    out[0] = x * math.sqrt(P_SIZE)


def project(index, factors, gradient, result=None):
    images, keypoints, universe = factors.shape
    block = pl.BlockSpec((1, keypoints, universe), lambda i, index: (index[0], 0, 0))
    whole = pl.BlockSpec((keypoints, universe), lambda i, index: (0, 0))
    in_specs = [block, whole]
    operands = [factors, gradient]
    aliases = {}
    if result is not None:
        in_specs.append(pl.BlockSpec(memory_space=pl.ANY))
        operands.append(result)
        aliases = {3: 0}
    return pl.pallas_call(
        project_kernel,
        out_shape=jax.ShapeDtypeStruct(factors.shape, jnp.float32),
        grid_spec=pltpu.PrefetchScalarGridSpec(
            num_scalar_prefetch=1, grid=(1,), in_specs=in_specs, out_specs=block
        ),
        input_output_aliases=aliases,
        compiler_params=pltpu.CompilerParams(vmem_limit_bytes=16 * MIB),
        cost_estimate=pl.CostEstimate(flops=1500000000, bytes_accessed=2000000, transcendentals=0),
        name="project",
    )(index, *operands)


def shards(affinity, tile_pairs, factors):
    images, keypoints, universe = factors.shape
    tiles = affinity.shape[0]
    owner = lax.axis_index("tiles")
    turn = lax.axis_index("rep")
    first = tile_pairs[:, 0] - owner * images
    slot = tile_pairs[:, 1] - (owner - 1) * images
    swapped = jnp.where(slot < images, slot + 2 * images, jnp.where(slot < 2 * images, slot, slot - 2 * images))
    slot = jnp.where(owner % 2 == 0, slot, swapped)
    order = (turn + jnp.arange(images, dtype=jnp.int32)) % images
    meta = jnp.concatenate([first, slot, order]).astype(jnp.int32)

    rounded = factors.astype(jnp.bfloat16)
    from_across = across(rounded)
    from_mate = mate(rounded)

    wide = jax.ShapeDtypeStruct((images, keypoints, universe), jnp.float32)
    narrow = jax.ShapeDtypeStruct((images, keypoints, universe), jnp.bfloat16)
    one_wide = jax.ShapeDtypeStruct((keypoints, universe), jnp.float32)
    one = jax.ShapeDtypeStruct((keypoints, universe), jnp.bfloat16)

    own, to_mate, c0, c1, c2, c3 = pl.pallas_call(
        backward_kernel,
        out_shape=(wide, narrow, one_wide, one, one, one),
        in_specs=[SMEM, VMEM, VMEM],
        out_specs=(VMEM,) * 6,
        scratch_shapes=[pltpu.VMEM((3 * images, keypoints, universe), jnp.float32)],
        compiler_params=pltpu.CompilerParams(vmem_limit_bytes=24 * MIB),
        cost_estimate=pl.CostEstimate(flops=600000000, bytes_accessed=8000000, transcendentals=0),
        name="backward",
    )(meta, affinity, rounded)
    x1 = turned(c1, 1)
    x3 = turned(c3, -1)
    x2 = turned(c2, 2)
    terms = mate(to_mate)
    crossing = c0 + x1.astype(jnp.float32) + x2.astype(jnp.float32) + x3.astype(jnp.float32)
    crossed = across(crossing.astype(jnp.bfloat16))

    p0, p1, p2, p3 = pl.pallas_call(
        forward_kernel,
        out_shape=(one_wide, one, one, one),
        in_specs=[SMEM] + [VMEM] * 6,
        out_specs=(VMEM,) * 4,
        scratch_shapes=[
            pltpu.VMEM((keypoints, universe), jnp.bfloat16),
            pltpu.VMEM((images, keypoints, universe), jnp.float32),
        ],
        compiler_params=pltpu.CompilerParams(vmem_limit_bytes=24 * MIB),
        cost_estimate=pl.CostEstimate(flops=600000000, bytes_accessed=8000000, transcendentals=0),
        name="forward",
    )(meta, affinity, rounded, from_mate, from_across, own, terms)
    y1 = turned(p1, 1)
    y3 = turned(p3, -1)
    y2 = turned(p2, 2)
    gradient = p0 + y1.astype(jnp.float32) + y2.astype(jnp.float32) + y3.astype(jnp.float32) + crossed.astype(jnp.float32)
    gradient = gradient.astype(jnp.bfloat16)
    z1 = turned(gradient, 1)
    z3 = turned(gradient, -1)
    z2 = turned(gradient, 2)
    result = project(order[0:1], factors, gradient)
    result = project(order[3:4], factors, z1, result)
    result = project(order[1:2], factors, z3, result)
    result = project(order[2:3], factors, z2, result)
    return result


def solution(mesh):
    in_specs = (P(("tiles", "rep"), None, None), P(("tiles", "rep"), None), P("tiles", None, None))
    out_specs = P("tiles", None, None)
    return jax.shard_map(shards, mesh=mesh, in_specs=in_specs, out_specs=out_specs, check_vma=False)
```

```python
import functools
import math

import jax
import jax.numpy as jnp
from jax import lax
from jax.experimental import pallas as pl
from jax.experimental.pallas import tpu as pltpu
from jax.sharding import PartitionSpec as P


P_SIZE = 512
NS_STEPS = 6
WIDE_STEPS = 1

epsilon = 1e-06
start_scale = 0.25
ascent_step = 0.25


SMEM = pl.BlockSpec(memory_space=pltpu.SMEM)
VMEM = pl.BlockSpec(memory_space=pltpu.VMEM)
MIB = 1 << 20


def mate(x):
    n = lax.axis_size("tiles")
    return lax.ppermute(x, "tiles", [(i, i ^ 1) for i in range(n)])


def across(x):
    n = lax.axis_size("tiles")
    pairs = [(i, i + 1) for i in range(1, n - 1, 2)]
    return lax.ppermute(x, "tiles", pairs + [(b, a) for a, b in pairs])


def turned(x, by):
    n = lax.axis_size("rep")
    return lax.ppermute(x, "rep", [(i, (i + by) % n) for i in range(n)])


def dot(a, b, dims=((1,), (0,))):
    return lax.dot_general(a, b, (dims, ((), ())), preferred_element_type=jnp.float32)


TN = ((0,), (0,))
NT = ((1,), (1,))


def accumulate(acc, slot, fresh, term):
    acc[slot] = jnp.where(fresh, jnp.zeros_like(term), acc[slot]) + term


def backward_kernel(meta, affinity, rounded, own, to_mate, c0, c1, c2, c3, acc):
    tiles = affinity.shape[0]
    images = rounded.shape[0]
    slots = [meta[tiles + t] for t in range(tiles)]
    for t in range(tiles):
        fresh = slots[t] >= 0
        for u in range(t):
            fresh = jnp.logical_and(fresh, slots[u] != slots[t])
        accumulate(acc, slots[t], fresh, dot(affinity[t], rounded[meta[t]], TN))

    def total(slot):
        hit = slots[0] == slot
        for t in range(1, tiles):
            hit = jnp.logical_or(hit, slots[t] == slot)
        value = acc[slot]
        return jnp.where(hit, value, jnp.zeros_like(value))

    for k, ref in enumerate((c0, c1, c2, c3)):
        ref[...] = total(meta[2 * tiles + k]).astype(ref.dtype)
    for j in range(images):
        to_mate[j] = total(2 * images + j).astype(to_mate.dtype)
    for j in range(images):
        own[j] = total(images + j)


def forward_kernel(meta, affinity, rounded, from_mate, from_across, own, terms, p0, p1, p2, p3, rhs, acc):
    tiles = affinity.shape[0]
    images = rounded.shape[0]
    for j in range(images):
        acc[j] = own[j] + terms[j].astype(jnp.float32)
    for t in range(tiles):
        slot = meta[tiles + t]

        @pl.when(slot < images)
        def _():
            rhs[...] = from_across[slot]

        @pl.when(jnp.logical_and(slot >= images, slot < 2 * images))
        def _():
            rhs[...] = rounded[slot - images]

        @pl.when(slot >= 2 * images)
        def _():
            rhs[...] = from_mate[slot - 2 * images]

        first = meta[t]
        acc[first] = acc[first] + dot(affinity[t], rhs[...])
    for k, ref in enumerate((p0, p1, p2, p3)):
        ref[...] = acc[meta[2 * tiles + k]].astype(ref.dtype)


def split(x):
    high = x.astype(jnp.bfloat16)
    return high, (x - high.astype(jnp.float32)).astype(jnp.bfloat16)


def project_kernel(places, meta, factors, *rest):
    count = len(places)
    gradients = rest[:count]
    out, held, sems = rest[-3:]
    ys = []
    for place, gradient in zip(places, gradients):
        x = factors[meta[place]] + ascent_step * gradient[...].astype(jnp.float32)
        squares = jnp.sum(jnp.sum(x * x, axis=0, keepdims=True), axis=1, keepdims=True)
        x = x * (start_scale * math.sqrt(x.shape[1]) * lax.rsqrt(squares + epsilon))
        ys.append(x.T)
    for step in range(NS_STEPS):
        if step < NS_STEPS - WIDE_STEPS:
            highs = [y.astype(jnp.bfloat16) for y in ys]
            grams = [dot(h, h, NT).astype(jnp.bfloat16) for h in highs]
            changes = [dot(g, h) for g, h in zip(grams, highs)]
        else:
            halves = [split(y) for y in ys]
            mixed = [dot(high, low, NT) for high, low in halves]
            grams = [split(dot(high, high, NT) + (m + m.T)) for (high, low), m in zip(halves, mixed)]
            changes = [
                dot(gh, high) + (dot(gl, high) + dot(gh, low))
                for (gh, gl), (high, low) in zip(grams, halves)
            ]
        ys = [1.5 * y - 0.5 * c for y, c in zip(ys, changes)]
    copies = []
    for k, (place, y) in enumerate(zip(places, ys)):
        held[k] = (y * math.sqrt(P_SIZE)).T
        copies.append(pltpu.make_async_copy(held.at[k], out.at[meta[place]], sems.at[k]))
        copies[-1].start()
    for copy in copies:
        copy.wait()


def project(places, meta, factors, gradients, result=None):
    _, keypoints, universe = factors.shape
    count = len(places)
    in_specs = [SMEM, VMEM] + [VMEM] * count
    operands = [meta, factors, *gradients]
    aliases = {}
    if result is not None:
        aliases = {len(operands): 0}
        in_specs.append(pl.BlockSpec(memory_space=pl.ANY))
        operands.append(result)
    return pl.pallas_call(
        functools.partial(project_kernel, places),
        out_shape=jax.ShapeDtypeStruct(factors.shape, jnp.float32),
        in_specs=in_specs,
        out_specs=pl.BlockSpec(memory_space=pl.ANY),
        scratch_shapes=[
            pltpu.VMEM((count, keypoints, universe), jnp.float32),
            pltpu.SemaphoreType.DMA((count,)),
        ],
        input_output_aliases=aliases,
        compiler_params=pltpu.CompilerParams(vmem_limit_bytes=16 * MIB),
        cost_estimate=pl.CostEstimate(flops=count * 2000000000, bytes_accessed=count * 2000000, transcendentals=0),
        name="project",
    )(*operands)


def shards(affinity, tile_pairs, factors):
    images, keypoints, universe = factors.shape
    tiles = affinity.shape[0]
    owner = lax.axis_index("tiles")
    turn = lax.axis_index("rep")
    first = tile_pairs[:, 0] - owner * images
    slot = tile_pairs[:, 1] - (owner - 1) * images
    swapped = jnp.where(slot < images, slot + 2 * images, jnp.where(slot < 2 * images, slot, slot - 2 * images))
    slot = jnp.where(owner % 2 == 0, slot, swapped)
    order = (turn + jnp.arange(images, dtype=jnp.int32)) % images
    meta = jnp.concatenate([first, slot, order]).astype(jnp.int32)

    rounded = factors.astype(jnp.bfloat16)
    rounded, meta = lax.optimization_barrier((rounded, meta))
    from_across = across(rounded)

    wide = jax.ShapeDtypeStruct((images, keypoints, universe), jnp.float32)
    narrow = jax.ShapeDtypeStruct((images, keypoints, universe), jnp.bfloat16)
    one_wide = jax.ShapeDtypeStruct((keypoints, universe), jnp.float32)
    one = jax.ShapeDtypeStruct((keypoints, universe), jnp.bfloat16)

    own, to_mate, c0, c1, c2, c3 = pl.pallas_call(
        backward_kernel,
        out_shape=(wide, narrow, one_wide, one, one, one),
        in_specs=[SMEM, VMEM, VMEM],
        out_specs=(VMEM,) * 6,
        scratch_shapes=[pltpu.VMEM((3 * images, keypoints, universe), jnp.float32)],
        compiler_params=pltpu.CompilerParams(vmem_limit_bytes=12 * MIB),
        cost_estimate=pl.CostEstimate(flops=600000000, bytes_accessed=8000000, transcendentals=0),
        name="backward",
    )(meta, affinity, rounded)
    x1 = turned(c1, 1)
    x3 = turned(c3, -1)
    x2 = turned(c2, 2)
    from_mate = mate(rounded)
    terms = mate(to_mate)
    p0, p1, p2, p3 = pl.pallas_call(
        forward_kernel,
        out_shape=(one_wide, one, one, one),
        in_specs=[SMEM] + [VMEM] * 6,
        out_specs=(VMEM,) * 4,
        scratch_shapes=[
            pltpu.VMEM((keypoints, universe), jnp.bfloat16),
            pltpu.VMEM((images, keypoints, universe), jnp.float32),
        ],
        compiler_params=pltpu.CompilerParams(vmem_limit_bytes=12 * MIB),
        cost_estimate=pl.CostEstimate(flops=600000000, bytes_accessed=8000000, transcendentals=0),
        name="forward",
    )(meta, affinity, rounded, from_mate, from_across, own, terms)
    crossing = c0 + x1.astype(jnp.float32) + x2.astype(jnp.float32) + x3.astype(jnp.float32)
    crossed = across(crossing.astype(jnp.bfloat16))
    y1 = turned(p1, 1)
    y3 = turned(p3, -1)
    y2 = turned(p2, 2)
    gradient = p0 + y1.astype(jnp.float32) + y2.astype(jnp.float32) + y3.astype(jnp.float32) + crossed.astype(jnp.float32)
    gradient = gradient.astype(jnp.bfloat16)
    z1 = turned(gradient, 1)
    z3 = turned(gradient, -1)
    z2 = turned(gradient, 2)
    own_place = 2 * tiles
    result = project((own_place,), meta, factors, (gradient,))
    result = project((own_place + 3, own_place + 1), meta, factors, (z1, z3), result)
    result = project((own_place + 2,), meta, factors, (z2,), result)
    return result


def solution(mesh):
    in_specs = (P(("tiles", "rep"), None, None), P(("tiles", "rep"), None), P("tiles", None, None))
    out_specs = P("tiles", None, None)

    def step(*arguments):
        return shards(*arguments)

    step = jax.shard_map(step, mesh=mesh, in_specs=in_specs, out_specs=out_specs, check_vma=False)
    return step
```

```python
import functools
import math

import jax
import jax.numpy as jnp
from jax import lax
from jax.experimental import pallas as pl
from jax.experimental.pallas import tpu as pltpu
from jax.sharding import PartitionSpec as P


P_SIZE = 512
NS_STEPS = 6
WIDE_STEPS = 1

epsilon = 1e-06
start_scale = 0.25
ascent_step = 0.25


SMEM = pl.BlockSpec(memory_space=pltpu.SMEM)
VMEM = pl.BlockSpec(memory_space=pltpu.VMEM)
MIB = 1 << 20


def mate(x):
    n = lax.axis_size("tiles")
    return lax.ppermute(x, "tiles", [(i, i ^ 1) for i in range(n)])


def across(x):
    n = lax.axis_size("tiles")
    pairs = [(i, i + 1) for i in range(1, n - 1, 2)]
    return lax.ppermute(x, "tiles", pairs + [(b, a) for a, b in pairs])


def turned(x, by):
    n = lax.axis_size("rep")
    return lax.ppermute(x, "rep", [(i, (i + by) % n) for i in range(n)])


def dot(a, b, dims=((1,), (0,))):
    return lax.dot_general(a, b, (dims, ((), ())), preferred_element_type=jnp.float32)


TN = ((0,), (0,))
NT = ((1,), (1,))


def backward_kernel(meta, affinity, left, right, own_left, own_right, to_mate, c0, c1, c2, c3, acc):
    tiles = affinity.shape[0]
    images = left.shape[0]
    half = left.shape[2]
    slots = [meta[tiles + t] for t in range(tiles)]
    for t in range(tiles):
        fresh = slots[t] >= 0
        for u in range(t):
            fresh = jnp.logical_and(fresh, slots[u] != slots[t])
        first = jnp.concatenate([left[meta[t]], right[meta[t]]], axis=1)
        term = dot(affinity[t], first, TN)
        acc[slots[t]] = jnp.where(fresh, jnp.zeros_like(term), acc[slots[t]]) + term

    def total(slot):
        hit = slots[0] == slot
        for t in range(1, tiles):
            hit = jnp.logical_or(hit, slots[t] == slot)
        value = acc[slot]
        return jnp.where(hit, value, jnp.zeros_like(value))

    for k, ref in enumerate((c0, c1, c2, c3)):
        ref[...] = total(meta[2 * tiles + k]).astype(ref.dtype)
    for j in range(images):
        to_mate[j] = total(2 * images + j).astype(to_mate.dtype)
    for j in range(images):
        value = total(images + j)
        own_left[j] = value[:, :half]
        own_right[j] = value[:, half:]


def forward_kernel(start, meta, affinity, rounded, from_mate, from_across, own, terms, p0, p1, p2, p3, rhs, acc):
    tiles = affinity.shape[0]
    images, _, half = rounded.shape
    for j in range(images):
        acc[j] = own[j] + terms[j, :, start : start + half].astype(jnp.float32)
    for t in range(tiles):
        slot = meta[tiles + t]

        @pl.when(slot < images)
        def _():
            rhs[t] = from_across[slot]

        @pl.when(jnp.logical_and(slot >= images, slot < 2 * images))
        def _():
            rhs[t] = rounded[slot - images]

        @pl.when(slot >= 2 * images)
        def _():
            rhs[t] = from_mate[slot - 2 * images]

    for t in range(tiles):
        acc[meta[t]] = acc[meta[t]] + dot(affinity[t], rhs[t])
    for k, ref in enumerate((p0, p1, p2, p3)):
        ref[...] = acc[meta[2 * tiles + k]].astype(ref.dtype)


def round_kernel(wide, left, right):
    half = left.shape[2]
    left[...] = wide[:, :, :half].astype(left.dtype)
    right[...] = wide[:, :, half:].astype(right.dtype)


def sum_kernel(start, *refs):
    total = refs[0][...]
    width = total.shape[1]
    for ref in refs[1:-1]:
        part = ref[...] if ref.shape[1] == width else ref[:, start : start + width]
        total = total + part.astype(jnp.float32)
    refs[-1][...] = total.astype(refs[-1].dtype)


def split(x):
    high = x.astype(jnp.bfloat16)
    return high, (x - high.astype(jnp.float32)).astype(jnp.bfloat16)


def project_kernel(places, meta, factors, *rest):
    count = len(places)
    gradients = [jnp.concatenate([rest[2 * k][...], rest[2 * k + 1][...]], axis=1) for k in range(count)]
    out, held, sems = rest[-3:]
    ys = []
    for place, gradient in zip(places, gradients):
        x = factors[meta[place]] + ascent_step * gradient.astype(jnp.float32)
        squares = jnp.sum(jnp.sum(x * x, axis=0, keepdims=True), axis=1, keepdims=True)
        x = x * (start_scale * math.sqrt(x.shape[1]) * lax.rsqrt(squares + epsilon))
        ys.append(x.T)
    for step in range(NS_STEPS):
        if step < NS_STEPS - WIDE_STEPS:
            highs = [y.astype(jnp.bfloat16) for y in ys]
            grams = [dot(h, h, NT).astype(jnp.bfloat16) for h in highs]
            changes = [dot(g, h) for g, h in zip(grams, highs)]
        else:
            halves = [split(y) for y in ys]
            mixed = [dot(high, low, NT) for high, low in halves]
            grams = [split(dot(high, high, NT) + (m + m.T)) for (high, low), m in zip(halves, mixed)]
            changes = [
                dot(gh, high) + (dot(gl, high) + dot(gh, low))
                for (gh, gl), (high, low) in zip(grams, halves)
            ]
        ys = [1.5 * y - 0.5 * c for y, c in zip(ys, changes)]
    copies = []
    for k, (place, y) in enumerate(zip(places, ys)):
        held[k] = (y * math.sqrt(P_SIZE)).T
        copies.append(pltpu.make_async_copy(held.at[k], out.at[meta[place]], sems.at[k]))
        copies[-1].start()
    for copy in copies:
        copy.wait()


def project(places, meta, factors, gradients, result=None):
    _, keypoints, universe = factors.shape
    count = len(places)
    operands = [meta, factors]
    for pair in gradients:
        operands += pair
    in_specs = [SMEM] + [VMEM] * (len(operands) - 1)
    aliases = {}
    if result is not None:
        aliases = {len(operands): 0}
        in_specs.append(pl.BlockSpec(memory_space=pl.ANY))
        operands.append(result)
    return pl.pallas_call(
        functools.partial(project_kernel, places),
        out_shape=jax.ShapeDtypeStruct(factors.shape, jnp.float32),
        in_specs=in_specs,
        out_specs=pl.BlockSpec(memory_space=pl.ANY),
        scratch_shapes=[
            pltpu.VMEM((count, keypoints, universe), jnp.float32),
            pltpu.SemaphoreType.DMA((count,)),
        ],
        input_output_aliases=aliases,
        compiler_params=pltpu.CompilerParams(vmem_limit_bytes=16 * MIB),
        cost_estimate=pl.CostEstimate(flops=count * 2000000000, bytes_accessed=count * 2000000, transcendentals=0),
        name="project",
    )(*operands)


def shards(affinity, tile_pairs, factors):
    images, keypoints, universe = factors.shape
    tiles = affinity.shape[0]
    owner = lax.axis_index("tiles")
    turn = lax.axis_index("rep")
    first = tile_pairs[:, 0] - owner * images
    slot = tile_pairs[:, 1] - (owner - 1) * images
    swapped = jnp.where(slot < images, slot + 2 * images, jnp.where(slot < 2 * images, slot, slot - 2 * images))
    slot = jnp.where(owner % 2 == 0, slot, swapped)
    order = (turn + jnp.arange(images, dtype=jnp.int32)) % images
    meta = jnp.concatenate([first, slot, order]).astype(jnp.int32)

    half = universe // 2

    left, right = pl.pallas_call(
        round_kernel,
        out_shape=(jax.ShapeDtypeStruct((images, keypoints, half), jnp.bfloat16),) * 2,
        in_specs=[VMEM],
        out_specs=(VMEM, VMEM),
        compiler_params=pltpu.CompilerParams(vmem_limit_bytes=8 * MIB),
        name="rounded",
    )(factors)
    left, right, meta = lax.optimization_barrier((left, right, meta))
    across_left = across(left)
    across_right = across(right)

    def shape(*dims, dtype=jnp.bfloat16):
        return jax.ShapeDtypeStruct(dims, dtype)

    own_half = shape(images, keypoints, half, dtype=jnp.float32)
    own_left, own_right, to_mate, c0, c1, c2, c3 = pl.pallas_call(
        backward_kernel,
        out_shape=(
            own_half,
            own_half,
            shape(images, keypoints, universe),
            shape(keypoints, universe, dtype=jnp.float32),
        )
        + (shape(keypoints, universe),) * 3,
        in_specs=[SMEM, VMEM, VMEM, VMEM],
        out_specs=(VMEM,) * 7,
        scratch_shapes=[pltpu.VMEM((3 * images, keypoints, universe), jnp.float32)],
        compiler_params=pltpu.CompilerParams(vmem_limit_bytes=12 * MIB),
        cost_estimate=pl.CostEstimate(flops=600000000, bytes_accessed=8000000, transcendentals=0),
        name="backward",
    )(meta, affinity, left, right)
    x1 = turned(c1, 1)
    x3 = turned(c3, -1)
    x2 = turned(c2, 2)
    mate_left = mate(left)
    mate_right = mate(right)
    terms = mate(to_mate)

    def added(start, *operands):
        return pl.pallas_call(
            functools.partial(sum_kernel, start),
            out_shape=shape(*operands[0].shape),
            in_specs=[VMEM] * len(operands),
            out_specs=VMEM,
            compiler_params=pltpu.CompilerParams(vmem_limit_bytes=4 * MIB),
            cost_estimate=pl.CostEstimate(flops=1000000, bytes_accessed=1000000, transcendentals=0),
            name="added",
        )(*operands)

    crossed = across(added(0, c0, x1, x2, x3))

    def forward(start, *operands):
        return pl.pallas_call(
            functools.partial(forward_kernel, start),
            out_shape=(shape(keypoints, half, dtype=jnp.float32),) + (shape(keypoints, half),) * 3,
            in_specs=[SMEM] + [VMEM] * 6,
            out_specs=(VMEM,) * 4,
            scratch_shapes=[
                pltpu.VMEM((tiles, keypoints, half), jnp.bfloat16),
                pltpu.VMEM((images, keypoints, half), jnp.float32),
            ],
            compiler_params=pltpu.CompilerParams(vmem_limit_bytes=8 * MIB),
            cost_estimate=pl.CostEstimate(flops=600000000, bytes_accessed=4000000, transcendentals=0),
            name="forward",
        )(meta, affinity, *operands, terms)

    def scattered(parts):
        return parts[0], turned(parts[1], 1), turned(parts[3], -1), turned(parts[2], 2)

    def gathered(gradient):
        return [turned(gradient, 1), turned(gradient, -1), turned(gradient, 2)]

    left_parts = forward(0, left, mate_left, across_left, own_left)
    left_parts = scattered(left_parts)
    right_parts = forward(half, right, mate_right, across_right, own_right)
    right_parts = scattered(right_parts)
    left_sum = added(0, *left_parts[:1], crossed, *left_parts[1:])
    right_sum = added(half, *right_parts[:1], crossed, *right_parts[1:])
    zl = gathered(left_sum)
    zr = gathered(right_sum)
    own = 2 * tiles
    result = project((own,), meta, factors, [(left_sum, right_sum)])
    result = project((own + 3, own + 1, own + 2), meta, factors, list(zip(zl, zr)), result)
    return result


def solution(mesh):
    in_specs = (P(("tiles", "rep"), None, None), P(("tiles", "rep"), None), P("tiles", None, None))
    out_specs = P("tiles", None, None)

    def step(*arguments):
        return shards(*arguments)

    step = jax.shard_map(step, mesh=mesh, in_specs=in_specs, out_specs=out_specs, check_vma=False)
    return step
```

```python
import functools
import math

import jax
import jax.numpy as jnp
from jax import lax
from jax.experimental import pallas as pl
from jax.experimental.pallas import tpu as pltpu
from jax.sharding import PartitionSpec as P


P_SIZE = 512
NS_STEPS = 6
WIDE_STEPS = 1

epsilon = 1e-06
start_scale = 0.25
ascent_step = 0.25


SMEM = pl.BlockSpec(memory_space=pltpu.SMEM)
VMEM = pl.BlockSpec(memory_space=pltpu.VMEM)
MIB = 1 << 20


def mate(x):
    n = lax.axis_size("tiles")
    return lax.ppermute(x, "tiles", [(i, i ^ 1) for i in range(n)])


def across(x):
    n = lax.axis_size("tiles")
    pairs = [(i, i + 1) for i in range(1, n - 1, 2)]
    return lax.ppermute(x, "tiles", pairs + [(b, a) for a, b in pairs])


def turned(x, by):
    n = lax.axis_size("rep")
    return lax.ppermute(x, "rep", [(i, (i + by) % n) for i in range(n)])


def dot(a, b, dims=((1,), (0,))):
    return lax.dot_general(a, b, (dims, ((), ())), preferred_element_type=jnp.float32)


def places(pairs, images):
    owner = lax.axis_index("tiles")
    tiles = pairs.shape[1]
    even = lax.rem(owner, 2) == 0
    firsts, slots = [], []
    for t in range(tiles):
        firsts.append(pairs[0, t] - owner * images)
        slot = pairs[1, t] - (owner - 1) * images
        shift = jnp.where(slot < images, 2 * images, jnp.where(slot < 2 * images, 0, -2 * images))
        slots.append(slot + jnp.where(even, 0, shift))
    return firsts, slots, order(images)


def order(images):
    turn = lax.axis_index("rep")
    return [lax.rem(turn + k, images) for k in range(images)]


TN = ((0,), (0,))
NT = ((1,), (1,))


def backward_kernel(pairs, affinity, left, right, own_left, own_right, to_mate, c0, c1, c2, c3, acc):
    tiles = affinity.shape[0]
    images, _, half = left.shape
    firsts, slots, turns = places(pairs, images)
    for t in range(tiles):
        fresh = slots[t] >= 0
        for u in range(t):
            fresh = jnp.logical_and(fresh, slots[u] != slots[t])
        first = jnp.concatenate([left[firsts[t]], right[firsts[t]]], axis=1)
        term = dot(affinity[t], first, TN)
        acc[slots[t]] = jnp.where(fresh, jnp.zeros_like(term), acc[slots[t]]) + term

    def total(slot):
        hit = slots[0] == slot
        for t in range(1, tiles):
            hit = jnp.logical_or(hit, slots[t] == slot)
        value = acc[slot]
        return jnp.where(hit, value, jnp.zeros_like(value))

    for turn, ref in zip(turns, (c0, c1, c2, c3)):
        ref[...] = total(turn).astype(ref.dtype)
    for j in range(images):
        to_mate[j] = total(2 * images + j).astype(to_mate.dtype)
    for j in range(images):
        value = total(images + j)
        own_left[j] = value[:, :half]
        own_right[j] = value[:, half:]


def forward_kernel(
    start, pairs, affinity, rounded, from_mate, from_across, own, terms, p0, p1, p2, p3, rhs, acc, held, sem
):
    tiles = affinity.shape[0]
    images, _, half = rounded.shape
    copy = pltpu.make_async_copy(pairs, held, sem)
    copy.start()
    for j in range(images):
        acc[j] = own[j] + terms[j, :, start : start + half].astype(jnp.float32)
    copy.wait()
    firsts, slots, turns = places(held, images)
    for t in range(tiles):
        slot = slots[t]

        @pl.when(slot < images)
        def _():
            rhs[t] = from_across[slot]

        @pl.when(jnp.logical_and(slot >= images, slot < 2 * images))
        def _():
            rhs[t] = rounded[slot - images]

        @pl.when(slot >= 2 * images)
        def _():
            rhs[t] = from_mate[slot - 2 * images]

    for t in range(tiles):
        acc[firsts[t]] = acc[firsts[t]] + dot(affinity[t], rhs[t])
    for turn, ref in zip(turns, (p0, p1, p2, p3)):
        ref[...] = acc[turn].astype(ref.dtype)


def round_kernel(wide, left, right):
    half = left.shape[2]
    left[...] = wide[:, :, :half].astype(left.dtype)
    right[...] = wide[:, :, half:].astype(right.dtype)


def sum_kernel(start, *refs):
    total = refs[0][...]
    width = total.shape[1]
    for ref in refs[1:-1]:
        part = ref[...] if ref.shape[1] == width else ref[:, start : start + width]
        total = total + part.astype(jnp.float32)
    refs[-1][...] = total.astype(refs[-1].dtype)


def split(x):
    high = x.astype(jnp.bfloat16)
    return high, (x - high.astype(jnp.float32)).astype(jnp.bfloat16)


def project_kernel(ahead, factors, *rest):
    count = len(ahead)
    turns = order(factors.shape[0])
    gradients = [jnp.concatenate([rest[2 * k][...], rest[2 * k + 1][...]], axis=1) for k in range(count)]
    out, held, sems = rest[-3:]
    ys = []
    for k, gradient in zip(ahead, gradients):
        x = factors[turns[k]] + ascent_step * gradient.astype(jnp.float32)
        squares = jnp.sum(jnp.sum(x * x, axis=0, keepdims=True), axis=1, keepdims=True)
        x = x * (start_scale * math.sqrt(x.shape[1]) * lax.rsqrt(squares + epsilon))
        ys.append(x.T)
    for step in range(NS_STEPS):
        if step < NS_STEPS - WIDE_STEPS:
            highs = [y.astype(jnp.bfloat16) for y in ys]
            grams = [dot(h, h, NT).astype(jnp.bfloat16) for h in highs]
            changes = [dot(g, h) for g, h in zip(grams, highs)]
        else:
            halves = [split(y) for y in ys]
            mixed = [dot(high, low, NT) for high, low in halves]
            grams = [split(dot(high, high, NT) + (m + m.T)) for (high, low), m in zip(halves, mixed)]
            changes = [
                dot(gh, high) + (dot(gl, high) + dot(gh, low))
                for (gh, gl), (high, low) in zip(grams, halves)
            ]
        ys = [1.5 * y - 0.5 * c for y, c in zip(ys, changes)]
    copies = []
    for k, y in enumerate(ys):
        held[k] = (y * math.sqrt(P_SIZE)).T
        copies.append(pltpu.make_async_copy(held.at[k], out.at[turns[ahead[k]]], sems.at[k]))
        copies[-1].start()
    for copy in copies:
        copy.wait()


def project(ahead, factors, gradients, result=None):
    _, keypoints, universe = factors.shape
    count = len(ahead)
    operands = [factors]
    for pair in gradients:
        operands += pair
    in_specs = [VMEM] * len(operands)
    aliases = {}
    if result is not None:
        aliases = {len(operands): 0}
        in_specs.append(pl.BlockSpec(memory_space=pl.ANY))
        operands.append(result)
    return pl.pallas_call(
        functools.partial(project_kernel, ahead),
        out_shape=jax.ShapeDtypeStruct(factors.shape, jnp.float32),
        in_specs=in_specs,
        out_specs=pl.BlockSpec(memory_space=pl.ANY),
        scratch_shapes=[
            pltpu.VMEM((count, keypoints, universe), jnp.float32),
            pltpu.SemaphoreType.DMA((count,)),
        ],
        input_output_aliases=aliases,
        compiler_params=pltpu.CompilerParams(vmem_limit_bytes=16 * MIB),
        cost_estimate=pl.CostEstimate(flops=count * 2000000000, bytes_accessed=count * 2000000, transcendentals=0),
        name="project",
    )(*operands)


def shards(affinity, tile_pairs, factors):
    images, keypoints, universe = factors.shape
    half = universe // 2
    pairs = tile_pairs.T
    left, right = pl.pallas_call(
        round_kernel,
        out_shape=(jax.ShapeDtypeStruct((images, keypoints, half), jnp.bfloat16),) * 2,
        in_specs=[VMEM],
        out_specs=(VMEM, VMEM),
        compiler_params=pltpu.CompilerParams(vmem_limit_bytes=8 * MIB),
        cost_estimate=pl.CostEstimate(flops=1000000, bytes_accessed=3000000, transcendentals=0),
        name="rounded",
    )(factors)
    across_left = across(left)
    across_right = across(right)

    def shape(*dims, dtype=jnp.bfloat16):
        return jax.ShapeDtypeStruct(dims, dtype)

    own_left, own_right, to_mate, c0, c1, c2, c3 = pl.pallas_call(
        backward_kernel,
        out_shape=(
            shape(images, keypoints, half, dtype=jnp.float32),
            shape(images, keypoints, half, dtype=jnp.float32),
            shape(images, keypoints, universe),
            shape(keypoints, universe, dtype=jnp.float32),
        )
        + (shape(keypoints, universe),) * 3,
        in_specs=[SMEM, VMEM, VMEM, VMEM],
        out_specs=(VMEM,) * 7,
        scratch_shapes=[pltpu.VMEM((3 * images, keypoints, universe), jnp.float32)],
        compiler_params=pltpu.CompilerParams(vmem_limit_bytes=12 * MIB),
        cost_estimate=pl.CostEstimate(flops=600000000, bytes_accessed=8000000, transcendentals=0),
        name="backward",
    )(pairs, affinity, left, right)
    x1 = turned(c1, 1)
    x3 = turned(c3, -1)
    x2 = turned(c2, 2)
    mate_left = mate(left)
    mate_right = mate(right)
    terms = mate(to_mate)

    def added(start, *operands):
        return pl.pallas_call(
            functools.partial(sum_kernel, start),
            out_shape=shape(*operands[0].shape),
            in_specs=[VMEM] * len(operands),
            out_specs=VMEM,
            compiler_params=pltpu.CompilerParams(vmem_limit_bytes=4 * MIB),
            cost_estimate=pl.CostEstimate(flops=1000000, bytes_accessed=1000000, transcendentals=0),
            name="added",
        )(*operands)

    crossed = across(added(0, c0, x1, x2, x3))

    def forward(start, *operands):
        return pl.pallas_call(
            functools.partial(forward_kernel, start),
            out_shape=(shape(keypoints, half, dtype=jnp.float32),) + (shape(keypoints, half),) * 3,
            in_specs=[pl.BlockSpec(memory_space=pl.ANY)] + [VMEM] * 6,
            out_specs=(VMEM,) * 4,
            scratch_shapes=[
                pltpu.VMEM((affinity.shape[0], keypoints, half), jnp.bfloat16),
                pltpu.VMEM((images, keypoints, half), jnp.float32),
                pltpu.SMEM(pairs.shape, jnp.int32),
                pltpu.SemaphoreType.DMA(()),
            ],
            compiler_params=pltpu.CompilerParams(vmem_limit_bytes=8 * MIB),
            cost_estimate=pl.CostEstimate(flops=600000000, bytes_accessed=4000000, transcendentals=0),
            name="forward",
        )(pairs, affinity, *operands, terms)

    def scattered(parts):
        return parts[0], turned(parts[1], 1), turned(parts[3], -1), turned(parts[2], 2)

    def gathered(gradient):
        return [turned(gradient, 1), turned(gradient, -1), turned(gradient, 2)]

    left_parts = forward(0, left, mate_left, across_left, own_left)
    left_parts = scattered(left_parts)
    right_parts = forward(half, right, mate_right, across_right, own_right)
    right_parts = scattered(right_parts)
    left_sum = added(0, *left_parts[:1], crossed, *left_parts[1:])
    right_sum = added(half, *right_parts[:1], crossed, *right_parts[1:])
    zl = gathered(left_sum)
    zr = gathered(right_sum)
    result = project((0,), factors, [(left_sum, right_sum)])
    result = project((3, 1, 2), factors, list(zip(zl, zr)), result)
    return result


def solution(mesh):
    in_specs = (P(("tiles", "rep"), None, None), P(("tiles", "rep"), None), P("tiles", None, None))
    out_specs = P("tiles", None, None)

    def step(*arguments):
        return shards(*arguments)

    step = jax.shard_map(step, mesh=mesh, in_specs=in_specs, out_specs=out_specs, check_vma=False)
    return step
```

```python
import functools
import math

import jax
import jax.numpy as jnp
from jax import lax
from jax.experimental import pallas as pl
from jax.experimental.pallas import tpu as pltpu
from jax.sharding import PartitionSpec as P


P_SIZE = 512
KEEP = (0.0, 0.0, 0.0, 0.5, 0.5, 1.0)

epsilon = 1e-06
start_scale = 0.25
ascent_step = 0.25


SMEM = pl.BlockSpec(memory_space=pltpu.SMEM)
VMEM = pl.BlockSpec(memory_space=pltpu.VMEM)
MIB = 1 << 20


def mate(x):
    n = lax.axis_size("tiles")
    return lax.ppermute(x, "tiles", [(i, i ^ 1) for i in range(n)])


def across(x):
    n = lax.axis_size("tiles")
    pairs = [(i, i + 1) for i in range(1, n - 1, 2)]
    return lax.ppermute(x, "tiles", pairs + [(b, a) for a, b in pairs])


def turned(x, by):
    n = lax.axis_size("rep")
    return lax.ppermute(x, "rep", [(i, (i + by) % n) for i in range(n)])


def dot(a, b, dims=((1,), (0,))):
    return lax.dot_general(a, b, (dims, ((), ())), preferred_element_type=jnp.float32)


def places(pairs, images):
    owner = lax.axis_index("tiles")
    tiles = pairs.shape[1]
    even = lax.rem(owner, 2) == 0
    firsts, slots = [], []
    for t in range(tiles):
        firsts.append(pairs[0, t] - owner * images)
        slot = pairs[1, t] - (owner - 1) * images
        shift = jnp.where(slot < images, 2 * images, jnp.where(slot < 2 * images, 0, -2 * images))
        slots.append(slot + jnp.where(even, 0, shift))
    return firsts, slots, order(images)


def order(images):
    turn = lax.axis_index("rep")
    return [lax.rem(turn + k, images) for k in range(images)]


TN = ((0,), (0,))
NT = ((1,), (1,))


def backward_kernel(pairs, affinity, left, right, own_left, own_right, to_mate, c0, c1, c2, c3, acc):
    tiles = affinity.shape[0]
    images, _, half = left.shape
    firsts, slots, turns = places(pairs, images)
    for t in range(tiles):
        fresh = slots[t] >= 0
        for u in range(t):
            fresh = jnp.logical_and(fresh, slots[u] != slots[t])
        first = jnp.concatenate([left[firsts[t]], right[firsts[t]]], axis=1)
        term = dot(affinity[t], first, TN)
        acc[slots[t]] = jnp.where(fresh, jnp.zeros_like(term), acc[slots[t]]) + term

    def total(slot):
        hit = slots[0] == slot
        for t in range(1, tiles):
            hit = jnp.logical_or(hit, slots[t] == slot)
        value = acc[slot]
        return jnp.where(hit, value, jnp.zeros_like(value))

    for turn, ref in zip(turns, (c0, c1, c2, c3)):
        ref[...] = total(turn).astype(ref.dtype)
    for j in range(images):
        to_mate[j] = total(2 * images + j).astype(to_mate.dtype)
    for j in range(images):
        value = total(images + j)
        own_left[j] = value[:, :half]
        own_right[j] = value[:, half:]


def forward_kernel(
    start, pairs, affinity, rounded, from_mate, from_across, own, terms, p0, p1, p2, p3, rhs, acc, held, sem
):
    tiles = affinity.shape[0]
    images, _, half = rounded.shape
    copy = pltpu.make_async_copy(pairs, held, sem)
    copy.start()
    for j in range(images):
        acc[j] = own[j] + terms[j, :, start : start + half].astype(jnp.float32)
    copy.wait()
    firsts, slots, turns = places(held, images)
    for t in range(tiles):
        slot = slots[t]

        @pl.when(slot < images)
        def _():
            rhs[t] = from_across[slot]

        @pl.when(jnp.logical_and(slot >= images, slot < 2 * images))
        def _():
            rhs[t] = rounded[slot - images]

        @pl.when(slot >= 2 * images)
        def _():
            rhs[t] = from_mate[slot - 2 * images]

    for t in range(tiles):
        acc[firsts[t]] = acc[firsts[t]] + dot(affinity[t], rhs[t])
    for turn, ref in zip(turns, (p0, p1, p2, p3)):
        ref[...] = acc[turn].astype(ref.dtype)


def round_kernel(wide, left, right):
    half = left.shape[2]
    left[...] = wide[:, :, :half].astype(left.dtype)
    right[...] = wide[:, :, half:].astype(right.dtype)


def sum_kernel(start, *refs):
    total = refs[0][...]
    width = total.shape[1]
    for ref in refs[1:-1]:
        part = ref[...] if ref.shape[1] == width else ref[:, start : start + width]
        total = total + part.astype(jnp.float32)
    refs[-1][...] = total.astype(refs[-1].dtype)


def same_index(size):
    return lax.broadcasted_iota(jnp.int32, (size, size), 0) == lax.broadcasted_iota(jnp.int32, (size, size), 1)


def project_kernel(ahead, factors, *rest):
    count = len(ahead)
    turns = order(factors.shape[0])
    gradients = [jnp.concatenate([rest[2 * k][...], rest[2 * k + 1][...]], axis=1) for k in range(count)]
    out, held, sems = rest[-3:]
    ys = []
    for k, gradient in zip(ahead, gradients):
        x = factors[turns[k]] + ascent_step * gradient.astype(jnp.float32)
        squares = jnp.sum(jnp.sum(x * x, axis=0, keepdims=True), axis=1, keepdims=True)
        x = x * (start_scale * math.sqrt(x.shape[1]) * lax.rsqrt(squares + epsilon))
        ys.append(x.T)
    diagonal = same_index(ys[0].shape[0])
    for keep in KEEP:
        highs = [y.astype(jnp.bfloat16) for y in ys]
        grams = [dot(h, h, NT) for h in highs]
        if keep:
            grams = [g - jnp.where(diagonal, keep, 0.0) for g in grams]
        changes = [dot(g.astype(jnp.bfloat16), h) for g, h in zip(grams, highs)]
        ys = [(1.5 - 0.5 * keep) * y - 0.5 * c for y, c in zip(ys, changes)]
    copies = []
    for k, y in enumerate(ys):
        held[k] = (y * math.sqrt(P_SIZE)).T
        copies.append(pltpu.make_async_copy(held.at[k], out.at[turns[ahead[k]]], sems.at[k]))
        copies[-1].start()
    for copy in copies:
        copy.wait()


def project(ahead, factors, gradients, result=None):
    _, keypoints, universe = factors.shape
    count = len(ahead)
    operands = [factors]
    for pair in gradients:
        operands += pair
    in_specs = [VMEM] * len(operands)
    aliases = {}
    if result is not None:
        aliases = {len(operands): 0}
        in_specs.append(pl.BlockSpec(memory_space=pl.ANY))
        operands.append(result)
    return pl.pallas_call(
        functools.partial(project_kernel, ahead),
        out_shape=jax.ShapeDtypeStruct(factors.shape, jnp.float32),
        in_specs=in_specs,
        out_specs=pl.BlockSpec(memory_space=pl.ANY),
        scratch_shapes=[
            pltpu.VMEM((count, keypoints, universe), jnp.float32),
            pltpu.SemaphoreType.DMA((count,)),
        ],
        input_output_aliases=aliases,
        compiler_params=pltpu.CompilerParams(vmem_limit_bytes=16 * MIB),
        cost_estimate=pl.CostEstimate(flops=count * 2000000000, bytes_accessed=count * 2000000, transcendentals=0),
        name="project",
    )(*operands)


def shards(affinity, tile_pairs, factors):
    images, keypoints, universe = factors.shape
    half = universe // 2
    pairs = tile_pairs.T
    left, right = pl.pallas_call(
        round_kernel,
        out_shape=(jax.ShapeDtypeStruct((images, keypoints, half), jnp.bfloat16),) * 2,
        in_specs=[VMEM],
        out_specs=(VMEM, VMEM),
        compiler_params=pltpu.CompilerParams(vmem_limit_bytes=8 * MIB),
        cost_estimate=pl.CostEstimate(flops=1000000, bytes_accessed=3000000, transcendentals=0),
        name="rounded",
    )(factors)
    across_left = across(left)
    across_right = across(right)

    def shape(*dims, dtype=jnp.bfloat16):
        return jax.ShapeDtypeStruct(dims, dtype)

    own_left, own_right, to_mate, c0, c1, c2, c3 = pl.pallas_call(
        backward_kernel,
        out_shape=(
            shape(images, keypoints, half, dtype=jnp.float32),
            shape(images, keypoints, half, dtype=jnp.float32),
            shape(images, keypoints, universe),
            shape(keypoints, universe, dtype=jnp.float32),
        )
        + (shape(keypoints, universe),) * 3,
        in_specs=[SMEM, VMEM, VMEM, VMEM],
        out_specs=(VMEM,) * 7,
        scratch_shapes=[pltpu.VMEM((3 * images, keypoints, universe), jnp.float32)],
        compiler_params=pltpu.CompilerParams(vmem_limit_bytes=12 * MIB),
        cost_estimate=pl.CostEstimate(flops=600000000, bytes_accessed=8000000, transcendentals=0),
        name="backward",
    )(pairs, affinity, left, right)
    x1 = turned(c1, 1)
    x3 = turned(c3, -1)
    x2 = turned(c2, 2)
    mate_left = mate(left)
    mate_right = mate(right)
    terms = mate(to_mate)

    def added(start, *operands):
        return pl.pallas_call(
            functools.partial(sum_kernel, start),
            out_shape=shape(*operands[0].shape),
            in_specs=[VMEM] * len(operands),
            out_specs=VMEM,
            compiler_params=pltpu.CompilerParams(vmem_limit_bytes=4 * MIB),
            cost_estimate=pl.CostEstimate(flops=1000000, bytes_accessed=1000000, transcendentals=0),
            name="added",
        )(*operands)

    crossed = across(added(0, c0, x1, x2, x3))

    def forward(start, *operands):
        return pl.pallas_call(
            functools.partial(forward_kernel, start),
            out_shape=(shape(keypoints, half, dtype=jnp.float32),) + (shape(keypoints, half),) * 3,
            in_specs=[pl.BlockSpec(memory_space=pl.ANY)] + [VMEM] * 6,
            out_specs=(VMEM,) * 4,
            scratch_shapes=[
                pltpu.VMEM((affinity.shape[0], keypoints, half), jnp.bfloat16),
                pltpu.VMEM((images, keypoints, half), jnp.float32),
                pltpu.SMEM(pairs.shape, jnp.int32),
                pltpu.SemaphoreType.DMA(()),
            ],
            compiler_params=pltpu.CompilerParams(vmem_limit_bytes=8 * MIB),
            cost_estimate=pl.CostEstimate(flops=600000000, bytes_accessed=4000000, transcendentals=0),
            name="forward",
        )(pairs, affinity, *operands, terms)

    def scattered(parts):
        return parts[0], turned(parts[1], 1), turned(parts[3], -1), turned(parts[2], 2)

    def gathered(gradient):
        return [turned(gradient, 1), turned(gradient, -1), turned(gradient, 2)]

    left_parts = forward(0, left, mate_left, across_left, own_left)
    left_parts = scattered(left_parts)
    right_parts = forward(half, right, mate_right, across_right, own_right)
    right_parts = scattered(right_parts)
    left_sum = added(0, *left_parts[:1], crossed, *left_parts[1:])
    right_sum = added(half, *right_parts[:1], crossed, *right_parts[1:])
    zl = gathered(left_sum)
    zr = gathered(right_sum)
    result = project((0,), factors, [(left_sum, right_sum)])
    result = project((3, 1, 2), factors, list(zip(zl, zr)), result)
    return result


def solution(mesh):
    in_specs = (P(("tiles", "rep"), None, None), P(("tiles", "rep"), None), P("tiles", None, None))
    out_specs = P("tiles", None, None)

    def step(*arguments):
        return shards(*arguments)

    step = jax.shard_map(step, mesh=mesh, in_specs=in_specs, out_specs=out_specs, check_vma=False)
    return step
```

```python
import functools
import math

import jax
import jax.numpy as jnp
from jax import lax
from jax.experimental import pallas as pl
from jax.experimental.pallas import tpu as pltpu
from jax.sharding import PartitionSpec as P


P_SIZE = 512
KEEP = (0.0, 0.0, 0.5, 0.5, 1.0)

epsilon = 1e-06
start_scale = 0.25
ascent_step = 0.25


SMEM = pl.BlockSpec(memory_space=pltpu.SMEM)
VMEM = pl.BlockSpec(memory_space=pltpu.VMEM)
MIB = 1 << 20


def mate(x):
    n = lax.axis_size("tiles")
    return lax.ppermute(x, "tiles", [(i, i ^ 1) for i in range(n)])


def across(x):
    n = lax.axis_size("tiles")
    pairs = [(i, i + 1) for i in range(1, n - 1, 2)]
    return lax.ppermute(x, "tiles", pairs + [(b, a) for a, b in pairs])


def turned(x, by):
    n = lax.axis_size("rep")
    return lax.ppermute(x, "rep", [(i, (i + by) % n) for i in range(n)])


def dot(a, b, dims=((1,), (0,))):
    return lax.dot_general(a, b, (dims, ((), ())), preferred_element_type=jnp.float32)


def places(pairs, images):
    owner = lax.axis_index("tiles")
    tiles = pairs.shape[1]
    even = lax.rem(owner, 2) == 0
    firsts, slots = [], []
    for t in range(tiles):
        firsts.append(pairs[0, t] - owner * images)
        slot = pairs[1, t] - (owner - 1) * images
        shift = jnp.where(slot < images, 2 * images, jnp.where(slot < 2 * images, 0, -2 * images))
        slots.append(slot + jnp.where(even, 0, shift))
    return firsts, slots, order(images)


def order(images):
    turn = lax.axis_index("rep")
    return [lax.rem(turn + k, images) for k in range(images)]


TN = ((0,), (0,))
NT = ((1,), (1,))


def backward_kernel(pairs, affinity, left, right, own_left, own_right, to_mate, c0, c1, c2, c3, acc):
    tiles = affinity.shape[0]
    images, _, half = left.shape
    firsts, slots, turns = places(pairs, images)
    for t in range(tiles):
        fresh = slots[t] >= 0
        for u in range(t):
            fresh = jnp.logical_and(fresh, slots[u] != slots[t])
        first = jnp.concatenate([left[firsts[t]], right[firsts[t]]], axis=1)
        term = dot(affinity[t], first, TN)
        acc[slots[t]] = jnp.where(fresh, jnp.zeros_like(term), acc[slots[t]]) + term

    def total(slot):
        hit = slots[0] == slot
        for t in range(1, tiles):
            hit = jnp.logical_or(hit, slots[t] == slot)
        value = acc[slot]
        return jnp.where(hit, value, jnp.zeros_like(value))

    for turn, ref in zip(turns, (c0, c1, c2, c3)):
        ref[...] = total(turn).astype(ref.dtype)
    for j in range(images):
        to_mate[j] = total(2 * images + j).astype(to_mate.dtype)
    for j in range(images):
        value = total(images + j)
        own_left[j] = value[:, :half]
        own_right[j] = value[:, half:]


def forward_kernel(
    start, pairs, affinity, rounded, from_mate, from_across, own, terms, p0, p1, p2, p3, acc, held, sem
):
    images, _, half = rounded.shape
    copy = pltpu.make_async_copy(pairs, held, sem)
    copy.start()
    for j in range(images):
        acc[j] = own[j] + terms[j, :, start : start + half].astype(jnp.float32)
    copy.wait()
    firsts, slots, turns = places(held, images)
    for t, (first, slot) in enumerate(zip(firsts, slots)):
        image = lax.rem(slot, images)
        second = jnp.where(
            slot < images, from_across[image], jnp.where(slot < 2 * images, rounded[image], from_mate[image])
        )
        acc[first] = acc[first] + dot(affinity[t], second)
    for turn, ref in zip(turns, (p0, p1, p2, p3)):
        ref[...] = acc[turn].astype(ref.dtype)


def round_kernel(wide, left, right):
    half = left.shape[2]
    left[...] = wide[:, :, :half].astype(left.dtype)
    right[...] = wide[:, :, half:].astype(right.dtype)


def sum_kernel(start, *refs):
    total = refs[0][...]
    width = total.shape[1]
    for ref in refs[1:-1]:
        part = ref[...] if ref.shape[1] == width else ref[:, start : start + width]
        total = total + part.astype(jnp.float32)
    refs[-1][...] = total.astype(refs[-1].dtype)


def same_index(size):
    return lax.broadcasted_iota(jnp.int32, (size, size), 0) == lax.broadcasted_iota(jnp.int32, (size, size), 1)


def project_kernel(ahead, factors, *rest):
    count = len(ahead)
    turns = order(factors.shape[0])
    gradients = [jnp.concatenate([rest[2 * k][...], rest[2 * k + 1][...]], axis=1) for k in range(count)]
    out, held, sems = rest[-3:]
    ys, scales = [], []
    for k, gradient in zip(ahead, gradients):
        x = factors[turns[k]] + ascent_step * gradient.astype(jnp.float32)
        ys.append(x.T)
        squares = jnp.sum(jnp.sum(x * x, axis=0, keepdims=True), axis=1, keepdims=True)
        scales.append(start_scale * math.sqrt(x.shape[1]) * lax.rsqrt(squares + epsilon))
    highs = [y.astype(jnp.bfloat16) for y in ys]
    grams = [dot(h, h, NT) * (scale * scale) for h, scale in zip(highs, scales)]
    changes = [dot(g.astype(jnp.bfloat16), h) for g, h in zip(grams, highs)]
    ys = [(1.5 * y - 0.5 * c) * scale for y, c, scale in zip(ys, changes, scales)]
    diagonal = same_index(ys[0].shape[0])
    for step, keep in enumerate(KEEP):
        gain = math.sqrt(P_SIZE) if step == len(KEEP) - 1 else 1.0
        highs = [y.astype(jnp.bfloat16) for y in ys]
        grams = [dot(h, h, NT) for h in highs]
        if keep:
            grams = [g - jnp.where(diagonal, keep, 0.0) for g in grams]
        changes = [dot(g.astype(jnp.bfloat16), h) for g, h in zip(grams, highs)]
        ys = [gain * (1.5 - 0.5 * keep) * y - gain * 0.5 * c for y, c in zip(ys, changes)]
    copies = []
    for k, y in enumerate(ys):
        held[k] = y.T
        copies.append(pltpu.make_async_copy(held.at[k], out.at[turns[ahead[k]]], sems.at[k]))
        copies[-1].start()
    for copy in copies:
        copy.wait()


def project(ahead, factors, gradients, result=None):
    _, keypoints, universe = factors.shape
    count = len(ahead)
    operands = [factors]
    for pair in gradients:
        operands += pair
    in_specs = [VMEM] * len(operands)
    aliases = {}
    if result is not None:
        aliases = {len(operands): 0}
        in_specs.append(pl.BlockSpec(memory_space=pl.ANY))
        operands.append(result)
    return pl.pallas_call(
        functools.partial(project_kernel, ahead),
        out_shape=jax.ShapeDtypeStruct(factors.shape, jnp.float32),
        in_specs=in_specs,
        out_specs=pl.BlockSpec(memory_space=pl.ANY),
        scratch_shapes=[
            pltpu.VMEM((count, keypoints, universe), jnp.float32),
            pltpu.SemaphoreType.DMA((count,)),
        ],
        input_output_aliases=aliases,
        compiler_params=pltpu.CompilerParams(vmem_limit_bytes=16 * MIB),
        cost_estimate=pl.CostEstimate(flops=count * 2000000000, bytes_accessed=count * 2000000, transcendentals=0),
        name="project",
    )(*operands)


def shards(affinity, tile_pairs, factors):
    images, keypoints, universe = factors.shape
    half = universe // 2
    pairs = tile_pairs.T
    left, right = pl.pallas_call(
        round_kernel,
        out_shape=(jax.ShapeDtypeStruct((images, keypoints, half), jnp.bfloat16),) * 2,
        in_specs=[VMEM],
        out_specs=(VMEM, VMEM),
        compiler_params=pltpu.CompilerParams(vmem_limit_bytes=8 * MIB),
        cost_estimate=pl.CostEstimate(flops=1000000, bytes_accessed=3000000, transcendentals=0),
        name="rounded",
    )(factors)
    across_left = across(left)
    across_right = across(right)

    def shape(*dims, dtype=jnp.bfloat16):
        return jax.ShapeDtypeStruct(dims, dtype)

    own_left, own_right, to_mate, c0, c1, c2, c3 = pl.pallas_call(
        backward_kernel,
        out_shape=(
            shape(images, keypoints, half, dtype=jnp.float32),
            shape(images, keypoints, half, dtype=jnp.float32),
            shape(images, keypoints, universe),
            shape(keypoints, universe, dtype=jnp.float32),
        )
        + (shape(keypoints, universe),) * 3,
        in_specs=[SMEM, VMEM, VMEM, VMEM],
        out_specs=(VMEM,) * 7,
        scratch_shapes=[pltpu.VMEM((3 * images, keypoints, universe), jnp.float32)],
        compiler_params=pltpu.CompilerParams(vmem_limit_bytes=12 * MIB),
        cost_estimate=pl.CostEstimate(flops=600000000, bytes_accessed=8000000, transcendentals=0),
        name="backward",
    )(pairs, affinity, left, right)
    x1 = turned(c1, 1)
    x3 = turned(c3, -1)
    x2 = turned(c2, 2)
    mate_left = mate(left)
    mate_right = mate(right)
    terms = mate(to_mate)

    def added(start, *operands):
        return pl.pallas_call(
            functools.partial(sum_kernel, start),
            out_shape=shape(*operands[0].shape),
            in_specs=[VMEM] * len(operands),
            out_specs=VMEM,
            compiler_params=pltpu.CompilerParams(vmem_limit_bytes=4 * MIB),
            cost_estimate=pl.CostEstimate(flops=1000000, bytes_accessed=1000000, transcendentals=0),
            name="added",
        )(*operands)

    crossed = across(added(0, c0, x1, x2, x3))

    def forward(start, *operands):
        return pl.pallas_call(
            functools.partial(forward_kernel, start),
            out_shape=(shape(keypoints, half, dtype=jnp.float32),) + (shape(keypoints, half),) * 3,
            in_specs=[pl.BlockSpec(memory_space=pl.ANY)] + [VMEM] * 6,
            out_specs=(VMEM,) * 4,
            scratch_shapes=[
                pltpu.VMEM((images, keypoints, half), jnp.float32),
                pltpu.SMEM(pairs.shape, jnp.int32),
                pltpu.SemaphoreType.DMA(()),
            ],
            compiler_params=pltpu.CompilerParams(vmem_limit_bytes=8 * MIB),
            cost_estimate=pl.CostEstimate(flops=600000000, bytes_accessed=4000000, transcendentals=0),
            name="forward",
        )(pairs, affinity, *operands, terms)

    def scattered(parts):
        return parts[0], turned(parts[1], 1), turned(parts[3], -1), turned(parts[2], 2)

    def gathered(gradient):
        return [turned(gradient, 1), turned(gradient, -1), turned(gradient, 2)]

    left_parts = forward(0, left, mate_left, across_left, own_left)
    left_parts = scattered(left_parts)
    right_parts = forward(half, right, mate_right, across_right, own_right)
    right_parts = scattered(right_parts)
    left_sum = added(0, *left_parts[:1], crossed, *left_parts[1:])
    right_sum = added(half, *right_parts[:1], crossed, *right_parts[1:])
    zl = gathered(left_sum)
    zr = gathered(right_sum)
    result = project((0,), factors, [(left_sum, right_sum)])
    result = project((3, 1, 2), factors, list(zip(zl, zr)), result)
    return result


def solution(mesh):
    in_specs = (P(("tiles", "rep"), None, None), P(("tiles", "rep"), None), P("tiles", None, None))
    out_specs = P("tiles", None, None)

    def step(*arguments):
        return shards(*arguments)

    step = jax.shard_map(step, mesh=mesh, in_specs=in_specs, out_specs=out_specs, check_vma=False)
    return step
```

```python
import functools
import math

import jax
import jax.numpy as jnp
from jax import lax
from jax.experimental import pallas as pl
from jax.experimental.pallas import tpu as pltpu
from jax.sharding import PartitionSpec as P


P_SIZE = 512
KEEP = (0.0, 0.0, 0.5, 0.5, 1.0)

epsilon = 1e-06
start_scale = 0.25
ascent_step = 0.25


SMEM = pl.BlockSpec(memory_space=pltpu.SMEM)
VMEM = pl.BlockSpec(memory_space=pltpu.VMEM)
MIB = 1 << 20


def mate(x):
    n = lax.axis_size("tiles")
    return lax.ppermute(x, "tiles", [(i, i ^ 1) for i in range(n)])


def across(x):
    n = lax.axis_size("tiles")
    pairs = [(i, i + 1) for i in range(1, n - 1, 2)]
    return lax.ppermute(x, "tiles", pairs + [(b, a) for a, b in pairs])


def turned(x, by):
    n = lax.axis_size("rep")
    return lax.ppermute(x, "rep", [(i, (i + by) % n) for i in range(n)])


def dot(a, b, dims=((1,), (0,))):
    return lax.dot_general(a, b, (dims, ((), ())), preferred_element_type=jnp.float32)


def places(pairs, images):
    owner = lax.axis_index("tiles")
    tiles = pairs.shape[1]
    even = lax.rem(owner, 2) == 0
    firsts, slots = [], []
    for t in range(tiles):
        firsts.append(pairs[0, t] - owner * images)
        slot = pairs[1, t] - (owner - 1) * images
        shift = jnp.where(slot < images, 2 * images, jnp.where(slot < 2 * images, 0, -2 * images))
        slots.append(slot + jnp.where(even, 0, shift))
    return firsts, slots, order(images)


def order(images):
    turn = lax.axis_index("rep")
    return [lax.rem(turn + k, images) for k in range(images)]


TN = ((0,), (0,))
NT = ((1,), (1,))


def backward_kernel(pairs, affinity, left, right, sums, c0, c1, c2, c3, held, sem):
    tiles = affinity.shape[0]
    images = left.shape[0]
    copy = pltpu.make_async_copy(pairs, held, sem)
    copy.start()
    sums[...] = jnp.zeros_like(sums)
    copy.wait()
    firsts, slots, turns = places(held, images)
    for t in range(tiles):
        first = jnp.concatenate([left[firsts[t]], right[firsts[t]]], axis=1)
        sums[slots[t]] = sums[slots[t]] + dot(affinity[t], first, TN)
    for turn, ref in zip(turns, (c0, c1, c2, c3)):
        ref[...] = sums[turn].astype(ref.dtype)


def narrow_kernel(first, sums, out):
    for j in range(out.shape[0]):
        out[j] = sums[first + j].astype(out.dtype)


def forward_kernel(
    start, pairs, affinity, rounded, from_mate, from_across, own, terms, p0, p1, p2, p3, acc, held, sem
):
    images, _, half = rounded.shape
    copy = pltpu.make_async_copy(pairs, held, sem)
    copy.start()
    for j in range(images):
        acc[j] = own[images + j, :, start : start + half] + terms[j, :, start : start + half].astype(jnp.float32)
    copy.wait()
    firsts, slots, turns = places(held, images)
    for t, (first, slot) in enumerate(zip(firsts, slots)):
        image = lax.rem(slot, images)
        second = jnp.where(
            slot < images, from_across[image], jnp.where(slot < 2 * images, rounded[image], from_mate[image])
        )
        acc[first] = acc[first] + dot(affinity[t], second)
    for turn, ref in zip(turns, (p0, p1, p2, p3)):
        ref[...] = acc[turn].astype(ref.dtype)


def round_kernel(wide, left, right):
    half = left.shape[2]
    left[...] = wide[:, :, :half].astype(left.dtype)
    right[...] = wide[:, :, half:].astype(right.dtype)


def sum_kernel(start, *refs):
    total = refs[0][...]
    width = total.shape[1]
    for ref in refs[1:-1]:
        part = ref[...] if ref.shape[1] == width else ref[:, start : start + width]
        total = total + part.astype(jnp.float32)
    refs[-1][...] = total.astype(refs[-1].dtype)


def same_index(size):
    return lax.broadcasted_iota(jnp.int32, (size, size), 0) == lax.broadcasted_iota(jnp.int32, (size, size), 1)


def project_kernel(ahead, factors, *rest):
    count = len(ahead)
    turns = order(factors.shape[0])
    gradients = [jnp.concatenate([rest[2 * k][...], rest[2 * k + 1][...]], axis=1) for k in range(count)]
    out, held, sems = rest[-3:]
    ys, scales = [], []
    for k, gradient in zip(ahead, gradients):
        x = factors[turns[k]] + ascent_step * gradient.astype(jnp.float32)
        ys.append(x.T)
        squares = jnp.sum(jnp.sum(x * x, axis=0, keepdims=True), axis=1, keepdims=True)
        scales.append(start_scale * math.sqrt(x.shape[1]) * lax.rsqrt(squares + epsilon))
    highs = [y.astype(jnp.bfloat16) for y in ys]
    grams = [dot(h, h, NT) * (scale * scale) for h, scale in zip(highs, scales)]
    changes = [dot(g.astype(jnp.bfloat16), h) for g, h in zip(grams, highs)]
    ys = [(1.5 * y - 0.5 * c) * scale for y, c, scale in zip(ys, changes, scales)]
    diagonal = same_index(ys[0].shape[0])
    for step, keep in enumerate(KEEP):
        gain = math.sqrt(P_SIZE) if step == len(KEEP) - 1 else 1.0
        highs = [y.astype(jnp.bfloat16) for y in ys]
        grams = [dot(h, h, NT) for h in highs]
        if keep:
            grams = [g - jnp.where(diagonal, keep, 0.0) for g in grams]
        changes = [dot(g.astype(jnp.bfloat16), h) for g, h in zip(grams, highs)]
        ys = [gain * (1.5 - 0.5 * keep) * y - gain * 0.5 * c for y, c in zip(ys, changes)]
    copies = []
    for k, y in enumerate(ys):
        held[k] = y.T
        copies.append(pltpu.make_async_copy(held.at[k], out.at[turns[ahead[k]]], sems.at[k]))
        copies[-1].start()
    for copy in copies:
        copy.wait()


def project(ahead, factors, gradients, result=None):
    _, keypoints, universe = factors.shape
    count = len(ahead)
    operands = [factors]
    for pair in gradients:
        operands += pair
    in_specs = [VMEM] * len(operands)
    aliases = {}
    if result is not None:
        aliases = {len(operands): 0}
        in_specs.append(pl.BlockSpec(memory_space=pl.ANY))
        operands.append(result)
    return pl.pallas_call(
        functools.partial(project_kernel, ahead),
        out_shape=jax.ShapeDtypeStruct(factors.shape, jnp.float32),
        in_specs=in_specs,
        out_specs=pl.BlockSpec(memory_space=pl.ANY),
        scratch_shapes=[
            pltpu.VMEM((count, keypoints, universe), jnp.float32),
            pltpu.SemaphoreType.DMA((count,)),
        ],
        input_output_aliases=aliases,
        compiler_params=pltpu.CompilerParams(vmem_limit_bytes=16 * MIB),
        cost_estimate=pl.CostEstimate(flops=count * 2000000000, bytes_accessed=count * 2000000, transcendentals=0),
        name="project",
    )(*operands)


def shards(affinity, tile_pairs, factors):
    images, keypoints, universe = factors.shape
    half = universe // 2
    pairs = tile_pairs.T
    left, right = pl.pallas_call(
        round_kernel,
        out_shape=(jax.ShapeDtypeStruct((images, keypoints, half), jnp.bfloat16),) * 2,
        in_specs=[VMEM],
        out_specs=(VMEM, VMEM),
        compiler_params=pltpu.CompilerParams(vmem_limit_bytes=8 * MIB),
        cost_estimate=pl.CostEstimate(flops=1000000, bytes_accessed=3000000, transcendentals=0),
        name="rounded",
    )(factors)
    across_left = across(left)
    across_right = across(right)

    def shape(*dims, dtype=jnp.bfloat16):
        return jax.ShapeDtypeStruct(dims, dtype)

    sums, c0, c1, c2, c3 = pl.pallas_call(
        backward_kernel,
        out_shape=(
            shape(3 * images, keypoints, universe, dtype=jnp.float32),
            shape(keypoints, universe, dtype=jnp.float32),
        )
        + (shape(keypoints, universe),) * 3,
        in_specs=[pl.BlockSpec(memory_space=pl.ANY), VMEM, VMEM, VMEM],
        out_specs=(VMEM,) * 5,
        scratch_shapes=[pltpu.SMEM(pairs.shape, jnp.int32), pltpu.SemaphoreType.DMA(())],
        compiler_params=pltpu.CompilerParams(vmem_limit_bytes=8 * MIB),
        cost_estimate=pl.CostEstimate(flops=600000000, bytes_accessed=8000000, transcendentals=0),
        name="backward",
    )(pairs, affinity, left, right)
    to_mate = pl.pallas_call(
        functools.partial(narrow_kernel, 2 * images),
        out_shape=shape(images, keypoints, universe),
        in_specs=[VMEM],
        out_specs=VMEM,
        compiler_params=pltpu.CompilerParams(vmem_limit_bytes=4 * MIB),
        cost_estimate=pl.CostEstimate(flops=1000000, bytes_accessed=3000000, transcendentals=0),
        name="narrow",
    )(sums)
    x1 = turned(c1, 1)
    x3 = turned(c3, -1)
    x2 = turned(c2, 2)
    mate_left = mate(left)
    mate_right = mate(right)
    terms = mate(to_mate)

    def added(start, *operands):
        return pl.pallas_call(
            functools.partial(sum_kernel, start),
            out_shape=shape(*operands[0].shape),
            in_specs=[VMEM] * len(operands),
            out_specs=VMEM,
            compiler_params=pltpu.CompilerParams(vmem_limit_bytes=4 * MIB),
            cost_estimate=pl.CostEstimate(flops=1000000, bytes_accessed=1000000, transcendentals=0),
            name="added",
        )(*operands)

    crossed = across(added(0, c0, x1, x2, x3))

    def forward(start, *operands):
        return pl.pallas_call(
            functools.partial(forward_kernel, start),
            out_shape=(shape(keypoints, half, dtype=jnp.float32),) + (shape(keypoints, half),) * 3,
            in_specs=[pl.BlockSpec(memory_space=pl.ANY)] + [VMEM] * 6,
            out_specs=(VMEM,) * 4,
            scratch_shapes=[
                pltpu.VMEM((images, keypoints, half), jnp.float32),
                pltpu.SMEM(pairs.shape, jnp.int32),
                pltpu.SemaphoreType.DMA(()),
            ],
            compiler_params=pltpu.CompilerParams(vmem_limit_bytes=8 * MIB),
            cost_estimate=pl.CostEstimate(flops=600000000, bytes_accessed=4000000, transcendentals=0),
            name="forward",
        )(pairs, affinity, *operands, terms)

    def scattered(parts):
        return parts[0], turned(parts[1], 1), turned(parts[3], -1), turned(parts[2], 2)

    def gathered(gradient):
        return [turned(gradient, 1), turned(gradient, -1), turned(gradient, 2)]

    left_parts = forward(0, left, mate_left, across_left, sums)
    left_parts = scattered(left_parts)
    right_parts = forward(half, right, mate_right, across_right, sums)
    right_parts = scattered(right_parts)
    left_sum = added(0, *left_parts[:1], crossed, *left_parts[1:])
    right_sum = added(half, *right_parts[:1], crossed, *right_parts[1:])
    zl = gathered(left_sum)
    zr = gathered(right_sum)
    result = project((0,), factors, [(left_sum, right_sum)])
    result = project((3, 1, 2), factors, list(zip(zl, zr)), result)
    return result


def solution(mesh):
    in_specs = (P(("tiles", "rep"), None, None), P(("tiles", "rep"), None), P("tiles", None, None))
    out_specs = P("tiles", None, None)

    def step(*arguments):
        return shards(*arguments)

    step = jax.shard_map(step, mesh=mesh, in_specs=in_specs, out_specs=out_specs, check_vma=False)
    return step
```
